256 devices in a mesh: col: 32 (over x_hi, z, core), row: 8 (over x_lo, y).
Axes of the slice: x: 4 (x_hi: 2, x_lo: 2; x = x_hi * 2 + x_lo), y: 4, z: 8, core: 2. Of those that a mesh axis runs over, the one named last changes fastest.
Arguments:
- matrix: float32 [64, 64, 128, 128], P('col', 'row'), may hold values from -12 to 80, as said below
- col_owner: int32 [64], replicated, may hold values from 0 to 63, as said below
- row_owner: int32 [64], replicated, may hold values from 0 to 63, as said below
- pattern: int32 [2, 64], replicated, may hold values from 0 to 1, as said below
Outputs:
- factored: float32 [64, 64, 128, 128], P('col', 'row')
The draws below stay inside these ranges and needn't reach their ends.
Inputs may be any that keep to these rules, and one draw needn't show every extreme that they name: `col_owner`: a permutation of 0 to 63. `row_owner`: a permutation of 0 to 63. pattern[0, 1] is 1; pattern[k, i] is 0 for i <= k; pattern[1, i] >= pattern[0, i] for every i >= 2. `matrix`: the diagonal tile of every supernode is symmetric positive definite, and so is every diagonal tile after the updates.
All inputs are finite; a program needn't handle non-finite values.
Results may differ from the reference program's by a relative error of at most 0.0003.
Values sent between devices are 32-bit elements; how exact they have to be, the bound alone decides.
A program may use at most 64 MiB of HBM per device.

```python
import jax
import jax.numpy as jnp
from jax import lax

WIDTH = 128
NODES = 64


def owner_maps(key):
    col_map = jax.random.permutation(jax.random.fold_in(key, 11), NODES).astype(jnp.int32)
    row_map = jax.random.permutation(jax.random.fold_in(key, 13), NODES).astype(jnp.int32)
    return (col_map, row_map)


def draw_col_owner(key, part):
    return owner_maps(key)[0]


def draw_row_owner(key, part):
    return owner_maps(key)[1]


def draw_pattern(key, part):
    ordinal = jnp.arange(NODES, dtype=jnp.int32)
    first_rows = jax.random.randint(jax.random.fold_in(key, 17), (NODES,), 0, 2).astype(jnp.int32)
    extra_rows = (jax.random.randint(jax.random.fold_in(key, 19), (NODES,), 0, 4) == 0).astype(jnp.int32)
    first_rows = jnp.where(ordinal == 1, 1, jnp.where(ordinal < 1, 0, first_rows)).astype(jnp.int32)
    second_rows = jnp.where(ordinal <= 1, 0, jnp.maximum(first_rows, extra_rows)).astype(jnp.int32)
    return jnp.stack([first_rows, second_rows]).astype(jnp.int32)


def draw_matrix(key, part):
    col_map, row_map = owner_maps(key)
    full_shape = (NODES, NODES, WIDTH, WIDTH)
    base_noise = jax.random.normal(jax.random.fold_in(key, 23), full_shape, jnp.float32)
    diag_mark = jnp.zeros((NODES, NODES), jnp.float32).at[col_map, row_map].set(1.0)
    symmetric = (base_noise + jnp.swapaxes(base_noise, 2, 3)) * 0.85
    diag_lift = jax.random.uniform(jax.random.fold_in(key, 29), (NODES, NODES, WIDTH), jnp.float32, 56.0, 72.0)
    identity = jnp.eye(WIDTH, dtype=jnp.float32)
    diag_tiles = symmetric + diag_lift[..., None] * identity
    return jnp.where(diag_mark[:, :, None, None] > 0.5, diag_tiles, base_noise).astype(jnp.float32)


def setup_inputs(seed: int = 0) -> dict:
    arg_keys = jax.random.split(jax.random.key(seed), 5)
    matrix = draw_matrix(jax.random.fold_in(arg_keys[4], 71), 0)
    col_owner = draw_col_owner(jax.random.fold_in(arg_keys[4], 71), 0)
    row_owner = draw_row_owner(jax.random.fold_in(arg_keys[4], 71), 0)
    pattern = draw_pattern(jax.random.fold_in(arg_keys[4], 71), 0)
    return {"matrix": matrix, "col_owner": col_owner, "row_owner": row_owner, "pattern": pattern}


PRECISE = lax.Precision.HIGHEST

def panel_factors(column, diag_tile, kept_rows):
    lower_tri = jnp.linalg.cholesky(diag_tile)
    identity = jnp.eye(lower_tri.shape[0], dtype=lower_tri.dtype)
    inverse = lax.linalg.triangular_solve(lower_tri, identity, left_side=True, lower=True)
    scaled = jnp.einsum('spq,rq->spr', column, inverse, precision=PRECISE)
    return (lower_tri, jnp.where(kept_rows[:, None, None], scaled, jnp.zeros_like(scaled)))

def reference(matrix, col_owner, row_owner, pattern):
    node_count = matrix.shape[0]
    ordinal = jnp.arange(node_count, dtype=jnp.int32)
    col_node = jnp.zeros((node_count,), jnp.int32).at[col_owner].set(ordinal)
    row_node = jnp.zeros((node_count,), jnp.int32).at[row_owner].set(ordinal)
    for panel_id in range(2):
        position = col_owner[panel_id]
        column = matrix[position]
        diag_tile = column[row_owner[panel_id]]
        kept_rows = pattern[panel_id][row_node] == 1
        lower_tri, row_factors = panel_factors(column, diag_tile, kept_rows)
        col_factors = row_factors[row_owner[col_node]]

        def update(operands):
            column_tiles, factor, col_id = operands
            lower_half = row_node >= col_id
            product = jnp.einsum('spq,rq->spr', row_factors, factor, precision=PRECISE)
            return column_tiles - jnp.where(lower_half[:, None, None], product, jnp.zeros_like(product))
        matrix = lax.map(update, (matrix, col_factors, col_node))
        old_column = matrix[position]
        is_diag = row_node == panel_id
        new_column = jnp.where(is_diag[:, None, None], lower_tri[None], jnp.where(kept_rows[:, None, None], row_factors, old_column))
        matrix = matrix.at[position].set(new_column)
    return matrix
```

```python
import jax
import jax.numpy as jnp
from jax import lax
from jax.sharding import PartitionSpec as P

PRECISE = lax.Precision.HIGHEST


def owned_nodes(owner_map, first_place, how_many):
    places = first_place + jnp.arange(how_many, dtype=jnp.int32)
    ordinal = jnp.arange(owner_map.shape[0], dtype=jnp.int32)
    matches = owner_map[None, :] == places[:, None]
    return jnp.sum(jnp.where(matches, ordinal[None, :], 0), axis=1)


def diag_factor(diag_tile):
    lower_tri = jnp.linalg.cholesky(diag_tile)
    identity = jnp.eye(lower_tri.shape[0], dtype=lower_tri.dtype)
    return (lower_tri, lax.linalg.triangular_solve(lower_tri, identity, left_side=True, lower=True))


def times_transposed(tiles, right):
    return jnp.einsum("...pq,rq->...pr", tiles, right, precision=PRECISE)


def keep_where(mask, tiles):
    return jnp.where(mask[..., None, None], tiles, jnp.zeros_like(tiles))


def body(matrix, col_owner, row_owner, pattern):
    cols_here = matrix.shape[0]
    slots_here = matrix.shape[1]
    col_rank = lax.axis_index("col")
    row_rank = lax.axis_index("row")
    first_slot = row_rank * slots_here
    col_node = owned_nodes(col_owner, col_rank * cols_here, cols_here)
    row_node = owned_nodes(row_owner, first_slot, slots_here)
    source_slot = row_owner[col_node]

    def own_tile(panel_id, slot):
        position = col_owner[panel_id]
        here = (position // cols_here == col_rank) & (slot // slots_here == row_rank)
        return keep_where(here, matrix[position % cols_here, slot % slots_here])

    leading = jnp.stack([own_tile(0, row_owner[0]), own_tile(0, row_owner[1]), own_tile(1, row_owner[1])])
    leading = lax.psum(leading, ("col", "row"))

    columns = jnp.stack(
        [
            keep_where(col_owner[k] // cols_here == col_rank, matrix[col_owner[k] % cols_here])
            for k in range(2)
        ]
    )
    columns, leading = lax.optimization_barrier((columns, leading))
    columns = lax.psum(columns, "col")

    held = source_slot // slots_here == row_rank
    across = keep_where(held[None, :], jnp.take(columns, source_slot % slots_here, axis=1))
    across = lax.psum(across, "row")

    lower_0, inverse_0 = diag_factor(leading[0])
    kept_next = jnp.where(pattern[0, 1] == 1, 1.0, 0.0).astype(jnp.float32)
    link = times_transposed(leading[1], inverse_0) * kept_next
    lower_1, inverse_1 = diag_factor(leading[2] - times_transposed(link, link))

    def factors(raw, nodes):
        kept = pattern[:, nodes] == 1
        first = keep_where(kept[0], times_transposed(raw[0], inverse_0))
        second = raw[1] - keep_where(nodes >= 1, times_transposed(first, link))
        second = keep_where(kept[1], times_transposed(second, inverse_1))
        return first, second

    row_factors = factors(columns, row_node)
    col_factors = factors(across, col_node)
    product = jnp.einsum(
        "spq,lrq->lspr",
        jnp.concatenate(row_factors, axis=-1),
        jnp.concatenate(col_factors, axis=-1),
        precision=PRECISE,
    )
    lower_half = row_node[None, :] >= col_node[:, None]
    matrix = matrix - keep_where(lower_half, product)

    for panel_id, lower_tri in enumerate((lower_0, lower_1)):
        mine = (col_node == panel_id)[:, None]
        is_diag = mine & (row_node == panel_id)[None, :]
        is_kept = mine & (pattern[panel_id][row_node] == 1)[None, :]
        matrix = jnp.where(is_kept[..., None, None], row_factors[panel_id][None], matrix)
        matrix = jnp.where(is_diag[..., None, None], lower_tri, matrix)
    return matrix


def solution(mesh):
    return jax.shard_map(
        body,
        mesh=mesh,
        in_specs=(P("col", "row", None, None), P(), P(), P()),
        out_specs=P("col", "row", None, None),
        check_vma=False,
    )
```
